32 devices in a mesh: seq: 16 (over z, y, x), head: 2 (over core).
Axes of the slice: x: 2, y: 2, z: 4, core: 2. Of those that a mesh axis runs over, the one named last changes fastest.
Arguments:
- win_query: bfloat16 [4096, 4096], P('seq', 'head'), may hold values from -24 to 24
- win_key: bfloat16 [4096, 4096], P('seq', 'head'), may hold values from -24 to 24
- win_value: bfloat16 [4096, 4096], P('seq', 'head'), may hold values from -24 to 24
- clu_query: bfloat16 [4096, 4096], P('seq', 'head'), may hold values from -24 to 24
- clu_key: bfloat16 [4096, 4096], P('seq', 'head'), may hold values from -24 to 24
- clu_value: bfloat16 [4096, 4096], P('seq', 'head'), may hold values from -24 to 24
- cluster_ids: int32 [32, 4096], P('head', 'seq'), may hold values from 0 to 63, as said below
- win_gain: float32 [4096], P('head'), may hold values from 0.5 to 1.5
- clu_gain: float32 [4096], P('head'), may hold values from 0.5 to 1.5
- win_out_grad: bfloat16 [4096, 4096], P('seq', 'head'), may hold values from -9 to 9
- clu_out_grad: bfloat16 [4096, 4096], P('seq', 'head'), may hold values from -9 to 9
Outputs:
- win_normed: bfloat16 [4096, 4096], P('seq', 'head')
- clu_normed: bfloat16 [4096, 4096], P('seq', 'head')
- win_dq: bfloat16 [4096, 4096], P('seq', 'head')
- win_dk: bfloat16 [4096, 4096], P('seq', 'head')
- win_dv: bfloat16 [4096, 4096], P('seq', 'head')
- clu_dq: bfloat16 [4096, 4096], P('seq', 'head')
- clu_dk: bfloat16 [4096, 4096], P('seq', 'head')
- clu_dv: bfloat16 [4096, 4096], P('seq', 'head')
The draws below stay inside these ranges and needn't reach their ends.
Inputs may be any that keep to these rules, and one draw needn't show every extreme that they name: `cluster_ids`: in every cluster head each cluster holds at most 8 of the tokens of each aligned block of 256 positions, hence at most 128 tokens in all; in every head one cluster holds exactly 8 tokens of every block.
All inputs are finite; a program needn't handle non-finite values.
Results may differ from the reference program's by a relative error of at most 0.035.
Values may be sent and summed in bfloat16 or wider, within the bound.
A program may use at most 192 MiB of HBM per device.

```python
import jax
import jax.numpy as jnp
from jax import lax

HW = 32
HC = 32
DH = 128
WINDOW = 256
SLOTS = 128
TOK_DEV = 256
TOKENS = 4096
CAP = 8
CLUSTERS = 64


def base_field(key, layout):
    values = jax.random.truncated_normal(key, -6.0, 6.0, layout, jnp.float32)
    return values


def cluster_table(key):
    base_key = jax.random.fold_in(key, 11)
    n_blocks = TOKENS // TOK_DEV
    pool_size = CLUSTERS * CAP
    full_cluster = jax.random.randint(jax.random.fold_in(base_key, 1), (HC,), 0, CLUSTERS)
    key_list = jax.random.split(jax.random.fold_in(base_key, 2), HC * n_blocks)
    owners = jnp.repeat(full_cluster, n_blocks)

    def one_block(block_key, chosen):
        first_key = jax.random.fold_in(block_key, 1)
        second_key = jax.random.fold_in(block_key, 2)
        score_int = jax.random.permutation(first_key, pool_size).astype(jnp.int32)
        slot_ids = jnp.arange(pool_size, dtype=jnp.int32)
        score_int = jnp.where(slot_ids // CAP == chosen, -1 - slot_ids % CAP, score_int)
        order_rows = jnp.argsort(score_int, stable=True)[:TOK_DEV]
        return (jax.random.permutation(second_key, order_rows) // CAP).astype(jnp.int32)
    table_ids = jax.vmap(one_block)(key_list, owners)
    return table_ids.reshape(HC, TOKENS)


def window_pairs(key):
    queries = base_field(jax.random.fold_in(key, 31), (TOKENS, HW, DH))
    key_rows = base_field(jax.random.fold_in(key, 32), (TOKENS, HW, DH))
    return (queries.reshape(TOKENS, HW * DH), key_rows.reshape(TOKENS, HW * DH))


def cluster_pairs(key):
    queries = base_field(jax.random.fold_in(key, 21), (TOKENS, HC, DH))
    key_rows = base_field(jax.random.fold_in(key, 22), (TOKENS, HC, DH))
    return (queries.reshape(TOKENS, HC * DH), key_rows.reshape(TOKENS, HC * DH))


def shared_part(key, label, n_heads):
    return base_field(jax.random.fold_in(key, label + 10), (n_heads, DH))


def rising_values(key, label, n_heads):
    head_ramp = 1.0 + 2.0 * jnp.arange(n_heads, dtype=jnp.float32) / (n_heads - 1)
    common = shared_part(key, label, n_heads)
    values = base_field(jax.random.fold_in(key, label), (TOKENS, n_heads, DH)) + 0.15 * common[None]
    values = values * head_ramp[None, :, None]
    return values.reshape(TOKENS, n_heads * DH)


def leaning_grads(key, label, n_heads):
    common = shared_part(key, label, n_heads)
    noise_rows = base_field(jax.random.fold_in(key, label + 20), (TOKENS, n_heads, DH))
    grads = 0.6 * noise_rows + 0.8 * common[None]
    return grads.reshape(TOKENS, n_heads * DH)


def draw_win_query(key, part):
    return window_pairs(key)[0].astype(jnp.bfloat16)


def draw_win_key(key, part):
    return window_pairs(key)[1].astype(jnp.bfloat16)


def draw_win_value(key, part):
    return rising_values(key, 41, HW).astype(jnp.bfloat16)


def draw_clu_query(key, part):
    return cluster_pairs(key)[0].astype(jnp.bfloat16)


def draw_clu_key(key, part):
    return cluster_pairs(key)[1].astype(jnp.bfloat16)


def draw_clu_value(key, part):
    return rising_values(key, 42, HC).astype(jnp.bfloat16)


def draw_cluster_ids(key, part):
    return cluster_table(key)


def draw_win_out_grad(key, part):
    return leaning_grads(key, 41, HW).astype(jnp.bfloat16)


def draw_clu_out_grad(key, part):
    return leaning_grads(key, 42, HC).astype(jnp.bfloat16)


def setup_inputs(seed: int = 0) -> dict:
    streams_of = jax.random.split(jax.random.key(seed), 12)
    return {
        "win_query": draw_win_query(jax.random.fold_in(streams_of[11], 71), 0),
        "win_key": draw_win_key(jax.random.fold_in(streams_of[11], 71), 0),
        "win_value": draw_win_value(jax.random.fold_in(streams_of[11], 71), 0),
        "clu_query": draw_clu_query(jax.random.fold_in(streams_of[11], 71), 0),
        "clu_key": draw_clu_key(jax.random.fold_in(streams_of[11], 71), 0),
        "clu_value": draw_clu_value(jax.random.fold_in(streams_of[11], 71), 0),
        "cluster_ids": draw_cluster_ids(jax.random.fold_in(streams_of[11], 71), 0),
        "win_gain": jnp.clip(1.0 + 0.1 * jax.random.normal(streams_of[7], (HW * DH,), jnp.float32), 0.5, 1.5),
        "clu_gain": jnp.clip(1.0 + 0.1 * jax.random.normal(streams_of[8], (HC * DH,), jnp.float32), 0.5, 1.5),
        "win_out_grad": draw_win_out_grad(jax.random.fold_in(streams_of[11], 71), 0),
        "clu_out_grad": draw_clu_out_grad(jax.random.fold_in(streams_of[11], 71), 0),
    }


EPSILON = 1e-06

def to_bf16_f32(values):
    return lax.optimization_barrier(values.astype(jnp.bfloat16)).astype(jnp.float32)

def softmax_rows(scores, allowed):
    masked = jnp.where(allowed, scores, -jnp.inf)
    top_row = lax.optimization_barrier(jnp.max(masked, axis=-1, keepdims=True))
    summed = lax.optimization_barrier(jnp.sum(jnp.exp(masked - top_row), axis=-1, keepdims=True))
    return jnp.exp(masked - (top_row + jnp.log(summed)))

def window_layout(values):
    blocks = values.astype(jnp.float32).reshape(-1, TOK_DEV, DH)
    before = jnp.concatenate([jnp.zeros_like(blocks[:1]), blocks[:-1]], axis=0)
    return (blocks, jnp.concatenate([before, blocks], axis=1))

def window_mask():
    n_blocks = TOKENS // TOK_DEV
    block_ids = jnp.arange(n_blocks, dtype=jnp.int32)[:, None, None] * TOK_DEV
    query_pos = block_ids + jnp.arange(TOK_DEV, dtype=jnp.int32)[None, :, None]
    key_pos = block_ids - TOK_DEV + jnp.arange(2 * TOK_DEV, dtype=jnp.int32)[None, None, :]
    gap_pos = query_pos - key_pos
    return (gap_pos >= 0) & (gap_pos < WINDOW) & (key_pos >= 0)

def window_core(queries, key_rows, val_rows):
    q_blocks, _ = window_layout(queries)
    _, k_ext = window_layout(key_rows)
    _, v_ext = window_layout(val_rows)
    scores = jnp.einsum('bid,bjd->bij', q_blocks, k_ext) * DH ** (-0.5)
    attn_prob = softmax_rows(scores, window_mask())
    weights = to_bf16_f32(attn_prob)
    return (q_blocks, k_ext, v_ext, attn_prob, weights)

def window_forward(queries, key_rows, val_rows):
    _, _, v_ext, _, weights = window_core(queries, key_rows, val_rows)
    return jnp.einsum('bij,bjd->bid', weights, v_ext).astype(jnp.bfloat16).reshape(TOKENS, DH)

def fold_blocks(part):
    own_part = part[:, TOK_DEV:]
    later = jnp.concatenate([part[1:, :TOK_DEV], jnp.zeros_like(part[:1, :TOK_DEV])], axis=0)
    return (own_part + later).reshape(TOKENS, DH)

def window_backward(queries, key_rows, val_rows, grad_rows, outputs):
    q_blocks, k_ext, v_ext, attn_prob, weights = window_core(queries, key_rows, val_rows)
    g_blocks = grad_rows.astype(jnp.float32).reshape(-1, TOK_DEV, DH)
    row_dot = lax.optimization_barrier(jnp.sum(g_blocks * outputs.astype(jnp.float32).reshape(-1, TOK_DEV, DH), axis=-1, keepdims=True))
    slope_rows = jnp.einsum('bid,bjd->bij', g_blocks, v_ext)
    change = to_bf16_f32(attn_prob * (slope_rows - row_dot))
    factor = DH ** (-0.5)
    grad_q = (jnp.einsum('bij,bjd->bid', change, k_ext) * factor).astype(jnp.bfloat16).reshape(TOKENS, DH)
    key_part = jnp.einsum('bij,bid->bjd', change, q_blocks)
    val_part = jnp.einsum('bij,bid->bjd', weights, g_blocks)
    grad_k = (fold_blocks(key_part) * factor).astype(jnp.bfloat16)
    grad_v = fold_blocks(val_part).astype(jnp.bfloat16)
    return (grad_q, grad_k, grad_v)

def cluster_layout(cluster_row):
    order_rows = jnp.argsort(cluster_row, stable=True).astype(jnp.int32)
    counts = jax.ops.segment_sum(jnp.ones((TOKENS,), jnp.int32), cluster_row, num_segments=CLUSTERS)
    starts = (jnp.cumsum(counts) - counts).astype(jnp.int32)
    sorted_ids = cluster_row[order_rows]
    rank_in = jnp.arange(TOKENS, dtype=jnp.int32) - starts[sorted_ids]
    slot_of = (sorted_ids * SLOTS + rank_in).astype(jnp.int32)
    slot_table = jnp.full((CLUSTERS * SLOTS,), TOKENS, jnp.int32).at[slot_of].set(order_rows)
    token_slot = jnp.zeros((TOKENS,), jnp.int32).at[order_rows].set(slot_of)
    return (slot_table, token_slot)

def padded(values, slot_table):
    valid_rows = slot_table < TOKENS
    picked = jnp.take(values.astype(jnp.float32), jnp.minimum(slot_table, TOKENS - 1), axis=0)
    picked = jnp.where(valid_rows[:, None], picked, 0.0)
    return (picked.reshape(CLUSTERS, SLOTS, DH), valid_rows.reshape(CLUSTERS, SLOTS))

def cluster_core(queries, key_rows, val_rows, cluster_row):
    slot_table, token_slot = cluster_layout(cluster_row)
    q_pad, valid_rows = padded(queries, slot_table)
    k_pad, _ = padded(key_rows, slot_table)
    v_pad, _ = padded(val_rows, slot_table)
    scores = jnp.einsum('cid,cjd->cij', q_pad, k_pad) * DH ** (-0.5)
    row_pos = lax.broadcasted_iota(jnp.int32, (SLOTS, SLOTS), 0)
    col_pos = lax.broadcasted_iota(jnp.int32, (SLOTS, SLOTS), 1)
    allowed = valid_rows[:, None, :] & (col_pos <= row_pos)[None] | (col_pos == row_pos)[None]
    attn_prob = softmax_rows(scores, allowed)
    weights = to_bf16_f32(attn_prob)
    out_pad = jnp.einsum('cij,cjd->cid', weights, v_pad).astype(jnp.bfloat16)
    return (slot_table, token_slot, q_pad, k_pad, v_pad, attn_prob, weights, out_pad)

def cluster_forward(queries, key_rows, val_rows, cluster_row):
    parts = cluster_core(queries, key_rows, val_rows, cluster_row)
    return parts[7].reshape(-1, DH)[parts[1]]

def cluster_backward(queries, key_rows, val_rows, cluster_row, grad_rows):
    slot_table, token_slot, q_pad, k_pad, v_pad, attn_prob, weights, out_pad = cluster_core(queries, key_rows, val_rows, cluster_row)
    g_pad, _ = padded(grad_rows, slot_table)
    row_dot = lax.optimization_barrier(jnp.sum(g_pad * out_pad.astype(jnp.float32), axis=-1, keepdims=True))
    slope_rows = jnp.einsum('cid,cjd->cij', g_pad, v_pad)
    change = to_bf16_f32(attn_prob * (slope_rows - row_dot))
    factor = DH ** (-0.5)
    grad_q = (jnp.einsum('cij,cjd->cid', change, k_pad) * factor).astype(jnp.bfloat16)
    grad_k = (jnp.einsum('cij,cid->cjd', change, q_pad) * factor).astype(jnp.bfloat16)
    grad_v = jnp.einsum('cij,cid->cjd', weights, g_pad).astype(jnp.bfloat16)
    return (grad_q.reshape(-1, DH)[token_slot], grad_k.reshape(-1, DH)[token_slot], grad_v.reshape(-1, DH)[token_slot])

def by_head(values, n_heads):
    return values.reshape(TOKENS, n_heads, DH).transpose(1, 0, 2)

def by_token(values, n_heads):
    return values.transpose(1, 0, 2).reshape(TOKENS, n_heads * DH)

def reference(win_query, win_key, win_value, clu_query, clu_key, clu_value, cluster_ids, win_gain, clu_gain, win_out_grad, clu_out_grad):
    q_win, k_win, v_win = (by_head(win_query, HW), by_head(win_key, HW), by_head(win_value, HW))
    q_clu, k_clu, v_clu = (by_head(clu_query, HC), by_head(clu_key, HC), by_head(clu_value, HC))
    attn_win = lax.map(lambda packed: window_forward(*packed), (q_win, k_win, v_win))
    attn_clu = lax.map(lambda packed: cluster_forward(*packed), (q_clu, k_clu, v_clu, cluster_ids))
    flat_win = by_token(attn_win, HW).astype(jnp.float32)
    flat_clu = by_token(attn_clu, HC).astype(jnp.float32)
    feat_width = (HW + HC) * DH
    sq_total = lax.optimization_barrier(jnp.sum(flat_win * flat_win, axis=1)) + lax.optimization_barrier(jnp.sum(flat_clu * flat_clu, axis=1))
    inv_rms = 1.0 / jnp.sqrt(sq_total / feat_width + EPSILON)
    win_normed = (flat_win * inv_rms[:, None] * win_gain).astype(jnp.bfloat16)
    clu_normed = (flat_clu * inv_rms[:, None] * clu_gain).astype(jnp.bfloat16)
    grad_win = win_out_grad.astype(jnp.float32) * win_gain
    grad_clu = clu_out_grad.astype(jnp.float32) * clu_gain
    dot_total = lax.optimization_barrier(jnp.sum(grad_win * flat_win, axis=1)) + lax.optimization_barrier(jnp.sum(grad_clu * flat_clu, axis=1))
    coef_rows = inv_rms ** 3 * dot_total / feat_width
    dout_win = (inv_rms[:, None] * grad_win - coef_rows[:, None] * flat_win).astype(jnp.bfloat16)
    dout_clu = (inv_rms[:, None] * grad_clu - coef_rows[:, None] * flat_clu).astype(jnp.bfloat16)
    win_grads = lax.map(lambda packed: window_backward(*packed), (q_win, k_win, v_win, by_head(dout_win, HW), attn_win))
    clu_grads = lax.map(lambda packed: cluster_backward(*packed), (q_clu, k_clu, v_clu, cluster_ids, by_head(dout_clu, HC)))
    return (win_normed, clu_normed, by_token(win_grads[0], HW), by_token(win_grads[1], HW), by_token(win_grads[2], HW), by_token(clu_grads[0], HC), by_token(clu_grads[1], HC), by_token(clu_grads[2], HC))
```

```python
import functools

import jax
import jax.numpy as jnp
from jax import lax
from jax.experimental import pallas as pl
from jax.experimental.pallas import tpu as pltpu
from jax.sharding import PartitionSpec as P

HW = 32
HC = 32
DH = 128
WINDOW = 256
SLOTS = 128
CHUNKS = 2

EPSILON = 1e-06
F32 = jnp.float32
BF16 = jnp.bfloat16


def from_behind(block, axis, distance):
    devices = range(lax.axis_size(axis))
    route = [(i - distance, i) for i in devices if i - distance in devices]
    return lax.ppermute(block, axis, route)


def nt(a, b):
    return lax.dot_general(a, b, (((1,), (1,)), ((), ())), preferred_element_type=F32)


def tn(a, b):
    return lax.dot_general(a, b, (((0,), (0,)), ((), ())), preferred_element_type=F32)


def nn(a, b):
    return jnp.dot(a, b, preferred_element_type=F32)


def one_hot(slot_ref, pool):
    n = slot_ref.shape[-1]
    hit = lax.broadcasted_iota(jnp.int32, (pool, n), 0) == slot_ref[0]
    return jnp.where(hit, 1.0, 0.0).astype(BF16)


def normalized(scores, allowed):
    masked = jnp.where(allowed, scores, -jnp.inf)
    grown = jnp.exp(masked - jnp.max(masked, axis=-1, keepdims=True))
    return grown * (1.0 / jnp.sum(grown, axis=-1, keepdims=True))


def call(kernel, grid, in_specs, out_specs, out_shape, flops, size, **more):
    return pl.pallas_call(
        kernel,
        grid=grid,
        in_specs=in_specs,
        out_specs=out_specs,
        out_shape=out_shape,
        cost_estimate=pl.CostEstimate(flops=flops, bytes_accessed=size, transcendentals=0),
        compiler_params=pltpu.CompilerParams(vmem_limit_bytes=48 << 20),
        **more,
    )


def dispatch_kernel(*refs):
    slot_ref, value_refs, out_ref = refs[0], refs[1:-1], refs[-1]
    picked = one_hot(slot_ref, out_ref.shape[0])
    for i, ref in enumerate(value_refs):
        out_ref[:, i * DH : (i + 1) * DH] = nn(picked, ref[...]).astype(BF16)


def dispatch(slot_at, values, first, count, pool):
    n = slot_at.shape[-1]
    wide = len(values) * DH
    return call(
        dispatch_kernel,
        (count,),
        [pl.BlockSpec((1, 1, n), lambda h: (h + first, 0, 0))]
        + [pl.BlockSpec((n, DH), lambda h: (0, h + first)) for _ in values],
        pl.BlockSpec((pool, wide), lambda h: (0, h)),
        jax.ShapeDtypeStruct((pool, count * wide), BF16),
        2 * count * pool * n * wide,
        2 * count * (pool + n) * wide,
    )(slot_at, *values)


def collect_kernel(n_out, *refs):
    slot_ref, rows_ref, out_refs = refs[0], refs[1], refs[-n_out:]
    picked = one_hot(slot_ref, rows_ref.shape[0])
    merged = tn(picked, rows_ref[...]).astype(BF16)
    for i, ref in enumerate(out_refs):
        ref[...] = merged[:, i * DH : (i + 1) * DH]


def collect(slot_at, rows, first, count, n_out, earlier):
    n = slot_at.shape[-1]
    pool = rows.shape[0]
    heads = slot_at.shape[0]
    wide = n_out * DH
    return call(
        functools.partial(collect_kernel, n_out),
        (count,),
        [
            pl.BlockSpec((1, 1, n), lambda h: (h + first, 0, 0)),
            pl.BlockSpec((pool, wide), lambda h: (0, h)),
        ]
        + [pl.BlockSpec(memory_space=pl.ANY) for _ in earlier],
        [pl.BlockSpec((n, DH), lambda h: (0, h + first))] * n_out,
        [jax.ShapeDtypeStruct((n, heads * DH), BF16)] * n_out,
        2 * count * pool * n * wide,
        2 * count * (pool + n) * wide,
        input_output_aliases={2 + i: i for i in range(len(earlier))},
    )(slot_at, rows, *earlier)


class Rows:
    def __init__(self, sources, owned, cap):
        self.sources, self.owned, self.cap = sources, owned, cap
        self.aligned = cap % 8 == 0

    def selector(self, c):
        members = self.sources * self.cap
        layout = (members, members * self.owned)
        member = lax.broadcasted_iota(jnp.int32, layout, 0)
        row = lax.broadcasted_iota(jnp.int32, layout, 1)
        want = member // self.cap * (self.cap * self.owned) + c * self.cap + member % self.cap
        return jnp.where(row == want, 1.0, 0.0).astype(BF16)

    def split(self, rows):
        members = self.sources * self.cap
        if not self.aligned:
            return [nn(self.selector(c), rows).astype(BF16) for c in range(self.owned)]
        wide = rows.shape[1]
        four = rows.astype(F32).reshape(self.sources, self.owned, self.cap, wide)
        return [four[:, c].reshape(members, wide).astype(BF16) for c in range(self.owned)]

    def join(self, parts):
        wide = parts[0].shape[1]
        pool = self.sources * self.cap * self.owned
        if not self.aligned:
            total = jnp.zeros((pool, wide), F32)
            for c, part in enumerate(parts):
                total = total + tn(self.selector(c), part.astype(BF16))
            return total.astype(BF16)
        shaped = [p.reshape(self.sources, 1, self.cap, wide) for p in parts]
        return jnp.concatenate(shaped, axis=1).reshape(pool, wide).astype(BF16)


def cluster_allowed(live_ref, c, members):
    row = lax.broadcasted_iota(jnp.int32, (members, members), 0)
    col = lax.broadcasted_iota(jnp.int32, (members, members), 1)
    live = jnp.broadcast_to(live_ref[0, c : c + 1, :], (members, members)) > 0.5
    return (live & (col <= row)) | (col == row)


def owner_fwd_kernel(rows, factor, live_ref, qkv_ref, out_ref):
    members = rows.sources * rows.cap
    parts = []
    for c, qkv in enumerate(rows.split(qkv_ref[...])):
        q, k, v = qkv[:, :DH], qkv[:, DH : 2 * DH], qkv[:, 2 * DH :]
        prob = normalized(nt(q, k) * factor, cluster_allowed(live_ref, c, members))
        parts.append(nn(prob.astype(BF16), v))
    out_ref[...] = rows.join(parts)


def owner_bwd_kernel(rows, factor, live_ref, qkv_ref, attn_ref, grad_ref, out_ref):
    members = rows.sources * rows.cap
    attn_parts = rows.split(attn_ref[...])
    grad_parts = rows.split(grad_ref[...])
    parts = []
    for c, qkv in enumerate(rows.split(qkv_ref[...])):
        q, k, v = qkv[:, :DH], qkv[:, DH : 2 * DH], qkv[:, 2 * DH :]
        grad = grad_parts[c]
        row_dot = jnp.sum(grad.astype(F32) * attn_parts[c].astype(F32), axis=-1, keepdims=True)
        prob = normalized(nt(q, k) * factor, cluster_allowed(live_ref, c, members))
        change = (prob * (nt(grad, v) - row_dot)).astype(BF16)
        dq = nn(change, k) * factor
        dk = tn(change, q) * factor
        dv = tn(prob.astype(BF16), grad)
        parts.append(jnp.concatenate([dq, dk, dv], axis=1))
    out_ref[...] = rows.join(parts)


def owner_call(kernel, rows, factor, live, first, arrays, n_out):
    pool = arrays[0].shape[0]
    count = arrays[0].shape[1] // (3 * DH)
    members = rows.sources * rows.cap
    wides = [a.shape[1] // count for a in arrays]
    return call(
        functools.partial(kernel, rows, factor),
        (count,),
        [pl.BlockSpec((1, rows.owned, members), lambda h: (h + first, 0, 0))]
        + [pl.BlockSpec((pool, w), lambda h: (0, h)) for w in wides],
        pl.BlockSpec((pool, n_out * DH), lambda h: (0, h)),
        jax.ShapeDtypeStruct((pool, count * n_out * DH), BF16),
        12 * count * pool * members * DH,
        2 * count * pool * (sum(wides) + n_out * DH),
    )(live, *arrays)


def window_prob(factor, q, keys):
    n = q.shape[0]
    row = lax.broadcasted_iota(jnp.int32, (n, n + WINDOW), 0)
    col = lax.broadcasted_iota(jnp.int32, (n, n + WINDOW), 1)
    gap = row + WINDOW - col
    lowest = jnp.where(lax.axis_index("seq") > 0, 0, WINDOW)
    allowed = (gap >= 0) & (gap < WINDOW) & (col >= lowest)
    return normalized(nt(q, keys) * factor, allowed)


def window_fwd_kernel(factor, q_ref, kp_ref, k_ref, vp_ref, v_ref, out_ref):
    keys = jnp.concatenate([kp_ref[0], k_ref[...]], axis=0)
    vals = jnp.concatenate([vp_ref[0], v_ref[...]], axis=0)
    prob = window_prob(factor, q_ref[...], keys)
    out_ref[...] = nn(prob.astype(BF16), vals).astype(BF16)


def window_bwd_kernel(
    factor, q_ref, kp_ref, k_ref, vp_ref, v_ref, attn_ref, grad_ref, dq_ref, dk_ref, dv_ref, rim_ref
):
    q, grad = q_ref[...], grad_ref[...]
    keys = jnp.concatenate([kp_ref[0], k_ref[...]], axis=0)
    vals = jnp.concatenate([vp_ref[0], v_ref[...]], axis=0)
    prob = window_prob(factor, q, keys)
    row_dot = jnp.sum(grad.astype(F32) * attn_ref[...].astype(F32), axis=-1, keepdims=True)
    change = (prob * (nt(grad, vals) - row_dot)).astype(BF16)
    dq_ref[...] = (nn(change, keys) * factor).astype(BF16)
    dk = tn(change, q)
    dv = tn(prob.astype(BF16), grad)
    rim_ref[0] = dk[:WINDOW].astype(BF16)
    rim_ref[1] = dv[:WINDOW].astype(BF16)
    dk_ref[...] = dk[WINDOW:]
    dv_ref[...] = dv[WINDOW:]


def window_specs(n):
    here = pl.BlockSpec((n, DH), lambda h: (0, h))
    key = pl.BlockSpec((1, n, DH), lambda h: (0, 0, h))
    val = pl.BlockSpec((1, n, DH), lambda h: (1, 0, h))
    return here, key, val


def window_fwd(factor, query, key, value, before):
    n, wide = query.shape
    here, rim_key, rim_val = window_specs(n)
    return call(
        functools.partial(window_fwd_kernel, factor),
        (wide // DH,),
        [here, rim_key, here, rim_val, here],
        here,
        jax.ShapeDtypeStruct((n, wide), BF16),
        4 * n * 2 * n * wide,
        12 * n * wide,
    )(query, before, key, before, value)


def window_bwd(factor, query, key, value, before, attn, grad):
    n, wide = query.shape
    here, rim_key, rim_val = window_specs(n)
    return call(
        functools.partial(window_bwd_kernel, factor),
        (wide // DH,),
        [here, rim_key, here, rim_val, here, here, here],
        [here, here, here, pl.BlockSpec((2, n, DH), lambda h: (0, 0, h))],
        [
            jax.ShapeDtypeStruct((n, wide), BF16),
            jax.ShapeDtypeStruct((n, wide), F32),
            jax.ShapeDtypeStruct((n, wide), F32),
            jax.ShapeDtypeStruct((2, n, wide), BF16),
        ],
        10 * n * 2 * n * wide,
        28 * n * wide,
    )(query, before, key, before, value, attn, grad)


def body(
    win_query,
    win_key,
    win_value,
    clu_query,
    clu_key,
    clu_value,
    cluster_ids,
    win_gain,
    clu_gain,
    win_out_grad,
    clu_out_grad,
):
    n_rows = win_query.shape[0]
    factor = DH ** (-0.5)
    feat_width = (HW + HC) * DH
    sources = lax.axis_size("seq")
    n_cap = SLOTS // sources
    owned_count = 2 * n_rows // SLOTS
    pool_size = 2 * n_rows
    clu_heads = clu_query.shape[1] // DH
    rows = Rows(sources, owned_count, n_cap)

    def exchange(values):
        shaped = values.reshape(sources, pool_size // sources, values.shape[1])
        moved = lax.all_to_all(shaped, "seq", split_axis=0, concat_axis=0, tiled=True)
        return moved.reshape(values.shape)

    row_ids = lax.broadcasted_iota(jnp.int32, (n_rows, n_rows), 0)
    col_ids = lax.broadcasted_iota(jnp.int32, (n_rows, n_rows), 1)
    same_cluster = (cluster_ids[:, :, None] == cluster_ids[:, None, :]) & (col_ids < row_ids)
    rank_in = jnp.sum(same_cluster.astype(jnp.int32), axis=-1)
    slot_at = (cluster_ids * n_cap + rank_in)[:, None, :]

    n_clusters = sources * owned_count
    every = lax.broadcasted_iota(jnp.int32, (n_clusters, clu_heads, n_rows), 0)
    counts = jnp.sum((cluster_ids[None] == every).astype(F32), axis=-1)
    counts = counts.reshape(sources, owned_count, clu_heads)
    counts = lax.all_to_all(counts, "seq", split_axis=0, concat_axis=0, tiled=True)
    slot_pos = lax.broadcasted_iota(F32, (clu_heads, owned_count, sources, n_cap), 3)
    live = (slot_pos < counts.transpose(2, 1, 0)[..., None]).astype(F32)
    live = live.reshape(clu_heads, owned_count, sources * n_cap)

    chunks = CHUNKS if clu_heads % CHUNKS == 0 else 1
    per = clu_heads // chunks
    starts = [i * per for i in range(chunks)]

    held = [
        exchange(dispatch(slot_at, [clu_query, clu_key, clu_value], first, per, pool_size))
        for first in starts
    ]
    before = from_behind(jnp.stack([win_key, win_value]), "seq", 1)
    attn_win = window_fwd(factor, win_query, win_key, win_value, before)

    attn_held = [
        owner_call(owner_fwd_kernel, rows, factor, live, first, [qkv], 1)
        for first, qkv in zip(starts, held)
    ]
    attn_back = [exchange(part) for part in attn_held]
    attn_clu = ()
    for first, part in zip(starts, attn_back):
        attn_clu = collect(slot_at, part, first, per, 1, attn_clu)
    attn_clu = attn_clu[0]

    flat_win = attn_win.astype(F32)
    flat_clu = attn_clu.astype(F32)
    grad_win = win_out_grad.astype(F32) * win_gain
    grad_clu = clu_out_grad.astype(F32) * clu_gain
    totals = jnp.stack(
        [
            jnp.sum(flat_win * flat_win, axis=1) + jnp.sum(flat_clu * flat_clu, axis=1),
            jnp.sum(grad_win * flat_win, axis=1) + jnp.sum(grad_clu * flat_clu, axis=1),
        ]
    )
    totals = lax.psum(totals, "head")
    sq_total, dot_total = totals[0], totals[1]
    inv_rms = 1.0 / jnp.sqrt(sq_total / feat_width + EPSILON)
    coef_rows = inv_rms**3 * dot_total / feat_width
    dout_clu = (inv_rms[:, None] * grad_clu - coef_rows[:, None] * flat_clu).astype(BF16)
    dout_win = (inv_rms[:, None] * grad_win - coef_rows[:, None] * flat_win).astype(BF16)
    win_normed = (flat_win * inv_rms[:, None] * win_gain).astype(BF16)
    clu_normed = (flat_clu * inv_rms[:, None] * clu_gain).astype(BF16)

    grad_held = [
        exchange(dispatch(slot_at, [dout_clu], first, per, pool_size)) for first in starts
    ]
    win_dq, key_own, val_own, rim = window_bwd(
        factor, win_query, win_key, win_value, before, attn_win, dout_win
    )
    after_rim = from_behind(rim, "seq", -1)

    clu_grads = ()
    sent = [
        owner_call(owner_bwd_kernel, rows, factor, live, first, [qkv, part, grad], 3)
        for first, qkv, part, grad in zip(starts, held, attn_held, grad_held)
    ]
    home = [exchange(part) for part in sent]
    win_dk = ((key_own + after_rim[0]) * factor).astype(BF16)
    win_dv = (val_own + after_rim[1]).astype(BF16)
    for first, part in zip(starts, home):
        clu_grads = collect(slot_at, part, first, per, 3, clu_grads)
    return (win_normed, clu_normed, win_dq, win_dk, win_dv, *clu_grads)


def solution(mesh):
    return jax.shard_map(
        body,
        mesh=mesh,
        in_specs=(P("seq", "head"),) * 6
        + (P("head", "seq"), P("head"), P("head"))
        + (P("seq", "head"),) * 2,
        out_specs=(P("seq", "head"),) * 8,
        check_vma=False,
    )
```

```python
import functools

import jax
import jax.numpy as jnp
from jax import lax
from jax.experimental import pallas as pl
from jax.experimental.pallas import tpu as pltpu
from jax.sharding import PartitionSpec as P

HW = 32
HC = 32
DH = 128
WINDOW = 256
SLOTS = 128
CHUNKS = 2
EMPTY = 1000.0

EPSILON = 1e-06
F32 = jnp.float32
BF16 = jnp.bfloat16


def from_behind(block, axis, distance):
    devices = range(lax.axis_size(axis))
    route = [(i - distance, i) for i in devices if i - distance in devices]
    return lax.ppermute(block, axis, route)


def nt(a, b):
    return lax.dot_general(a, b, (((1,), (1,)), ((), ())), preferred_element_type=F32)


def tn(a, b):
    return lax.dot_general(a, b, (((0,), (0,)), ((), ())), preferred_element_type=F32)


def nn(a, b):
    return jnp.dot(a, b, preferred_element_type=F32)


def one_hot(slot_ref, pool):
    n = slot_ref.shape[-1]
    hit = lax.broadcasted_iota(jnp.int32, (pool, n), 0) == slot_ref[0]
    return jnp.where(hit, 1.0, 0.0).astype(BF16)


def normalized(scores, allowed):
    masked = jnp.where(allowed, scores, -jnp.inf)
    grown = jnp.exp(masked - jnp.max(masked, axis=-1, keepdims=True))
    return grown * (1.0 / jnp.sum(grown, axis=-1, keepdims=True))


def call(kernel, grid, in_specs, out_specs, out_shape, flops, size, **more):
    return pl.pallas_call(
        kernel,
        grid=grid,
        in_specs=in_specs,
        out_specs=out_specs,
        out_shape=out_shape,
        cost_estimate=pl.CostEstimate(flops=flops, bytes_accessed=size, transcendentals=0),
        compiler_params=pltpu.CompilerParams(vmem_limit_bytes=60 << 20),
        **more,
    )


def dispatch_kernel(mark, *refs):
    slot_ref, value_refs, out_ref = refs[0], refs[1:-1], refs[-1]
    picked = one_hot(slot_ref, out_ref.shape[0])
    for i, ref in enumerate(value_refs):
        moved = nn(picked, ref[...])
        if mark and i == len(value_refs) - 1:
            filled = nn(picked, jnp.ones(ref.shape, BF16))
            moved = jnp.where(filled > 0.5, moved, EMPTY)
        out_ref[:, i * DH : (i + 1) * DH] = moved.astype(BF16)


def dispatch(slot_at, values, first, count, pool, mark):
    n = slot_at.shape[-1]
    wide = len(values) * DH
    return call(
        functools.partial(dispatch_kernel, mark),
        (count,),
        [pl.BlockSpec((1, 1, n), lambda h: (h + first, 0, 0))]
        + [pl.BlockSpec((n, DH), lambda h: (0, h + first)) for _ in values],
        pl.BlockSpec((pool, wide), lambda h: (0, h)),
        jax.ShapeDtypeStruct((pool, count * wide), BF16),
        2 * count * pool * n * wide,
        2 * count * (pool + n) * wide,
    )(slot_at, *values)


def collect_kernel(n_out, *refs):
    slot_ref, rows_ref, out_refs = refs[0], refs[1], refs[-n_out:]
    picked = one_hot(slot_ref, rows_ref.shape[0])
    merged = tn(picked, rows_ref[...]).astype(BF16)
    for i, ref in enumerate(out_refs):
        ref[...] = merged[:, i * DH : (i + 1) * DH]


def collect(slot_at, rows, first, count, n_out, earlier):
    n = slot_at.shape[-1]
    pool = rows.shape[0]
    heads = slot_at.shape[0]
    wide = n_out * DH
    return call(
        functools.partial(collect_kernel, n_out),
        (count,),
        [
            pl.BlockSpec((1, 1, n), lambda h: (h + first, 0, 0)),
            pl.BlockSpec((pool, wide), lambda h: (0, h)),
        ]
        + [pl.BlockSpec(memory_space=pl.ANY) for _ in earlier],
        [pl.BlockSpec((n, DH), lambda h: (0, h + first))] * n_out,
        [jax.ShapeDtypeStruct((n, heads * DH), BF16)] * n_out,
        2 * count * pool * n * wide,
        2 * count * (pool + n) * wide,
        input_output_aliases={2 + i: i for i in range(len(earlier))},
    )(slot_at, rows, *earlier)


class Rows:
    def __init__(self, sources, owned, cap):
        self.sources, self.owned, self.cap = sources, owned, cap
        self.aligned = cap % 8 == 0

    def selector(self, c):
        members = self.sources * self.cap
        layout = (members, members * self.owned)
        member = lax.broadcasted_iota(jnp.int32, layout, 0)
        row = lax.broadcasted_iota(jnp.int32, layout, 1)
        want = member // self.cap * (self.cap * self.owned) + c * self.cap + member % self.cap
        return jnp.where(row == want, 1.0, 0.0).astype(BF16)

    def split(self, rows):
        members = self.sources * self.cap
        if not self.aligned:
            return [nn(self.selector(c), rows).astype(BF16) for c in range(self.owned)]
        wide = rows.shape[1]
        four = rows.astype(F32).reshape(self.sources, self.owned, self.cap, wide)
        return [four[:, c].reshape(members, wide).astype(BF16) for c in range(self.owned)]

    def join(self, parts):
        wide = parts[0].shape[1]
        pool = self.sources * self.cap * self.owned
        if not self.aligned:
            total = jnp.zeros((pool, wide), F32)
            for c, part in enumerate(parts):
                total = total + tn(self.selector(c), part.astype(BF16))
            return total.astype(BF16)
        shaped = [p.reshape(self.sources, 1, self.cap, wide) for p in parts]
        return jnp.concatenate(shaped, axis=1).reshape(pool, wide).astype(BF16)


def cluster_allowed(v):
    members = v.shape[0]
    lane = lax.broadcasted_iota(jnp.int32, (8, DH), 1)
    first = nt(jnp.where(lane == 0, 1.0, 0.0).astype(BF16), v)[:1]
    row = lax.broadcasted_iota(jnp.int32, (members, members), 0)
    col = lax.broadcasted_iota(jnp.int32, (members, members), 1)
    live = jnp.broadcast_to(first, (members, members)) < EMPTY / 2
    return (live & (col <= row)) | (col == row)


def owner_fwd_kernel(rows, factor, qkv_ref, out_ref):
    parts = []
    for qkv in rows.split(qkv_ref[...]):
        q, k, v = qkv[:, :DH], qkv[:, DH : 2 * DH], qkv[:, 2 * DH :]
        prob = normalized(nt(q, k) * factor, cluster_allowed(v))
        parts.append(nn(prob.astype(BF16), v))
    out_ref[...] = rows.join(parts)


def owner_bwd_kernel(rows, factor, qkv_ref, attn_ref, grad_ref, out_ref):
    attn_parts = rows.split(attn_ref[...])
    grad_parts = rows.split(grad_ref[...])
    parts = []
    for c, qkv in enumerate(rows.split(qkv_ref[...])):
        q, k, v = qkv[:, :DH], qkv[:, DH : 2 * DH], qkv[:, 2 * DH :]
        grad = grad_parts[c]
        row_dot = jnp.sum(grad.astype(F32) * attn_parts[c].astype(F32), axis=-1, keepdims=True)
        prob = normalized(nt(q, k) * factor, cluster_allowed(v))
        change = (prob * (nt(grad, v) - row_dot)).astype(BF16)
        dq = nn(change, k) * factor
        dk = tn(change, q) * factor
        dv = tn(prob.astype(BF16), grad)
        parts.append(jnp.concatenate([dq, dk, dv], axis=1))
    out_ref[...] = rows.join(parts)


def owner_call(kernel, rows, factor, arrays, n_out):
    pool = arrays[0].shape[0]
    count = arrays[0].shape[1] // (3 * DH)
    members = rows.sources * rows.cap
    wides = [a.shape[1] // count for a in arrays]
    return call(
        functools.partial(kernel, rows, factor),
        (count,),
        [pl.BlockSpec((pool, w), lambda h: (0, h)) for w in wides],
        pl.BlockSpec((pool, n_out * DH), lambda h: (0, h)),
        jax.ShapeDtypeStruct((pool, count * n_out * DH), BF16),
        12 * count * pool * members * DH,
        2 * count * pool * (sum(wides) + n_out * DH),
    )(*arrays)


def window_prob(factor, q, keys):
    n = q.shape[0]
    row = lax.broadcasted_iota(jnp.int32, (n, n + WINDOW), 0)
    col = lax.broadcasted_iota(jnp.int32, (n, n + WINDOW), 1)
    gap = row + WINDOW - col
    lowest = jnp.where(lax.axis_index("seq") > 0, 0, WINDOW)
    allowed = (gap >= 0) & (gap < WINDOW) & (col >= lowest)
    return normalized(nt(q, keys) * factor, allowed)


def window_fwd_kernel(factor, q_ref, kp_ref, k_ref, vp_ref, v_ref, out_ref):
    keys = jnp.concatenate([kp_ref[...], k_ref[...]], axis=0)
    vals = jnp.concatenate([vp_ref[...], v_ref[...]], axis=0)
    prob = window_prob(factor, q_ref[...], keys)
    out_ref[...] = nn(prob.astype(BF16), vals).astype(BF16)


def window_bwd_kernel(
    factor, q_ref, kp_ref, k_ref, vp_ref, v_ref, attn_ref, grad_ref, dq_ref, dk_ref, dv_ref, rim_key_ref, rim_val_ref
):
    q, grad = q_ref[...], grad_ref[...]
    keys = jnp.concatenate([kp_ref[...], k_ref[...]], axis=0)
    vals = jnp.concatenate([vp_ref[...], v_ref[...]], axis=0)
    prob = window_prob(factor, q, keys)
    row_dot = jnp.sum(grad.astype(F32) * attn_ref[...].astype(F32), axis=-1, keepdims=True)
    change = (prob * (nt(grad, vals) - row_dot)).astype(BF16)
    dq_ref[...] = (nn(change, keys) * factor).astype(BF16)
    dk = tn(change, q)
    dv = tn(prob.astype(BF16), grad)
    rim_key_ref[...] = dk[:WINDOW].astype(BF16)
    rim_val_ref[...] = dv[:WINDOW].astype(BF16)
    dk_ref[...] = dk[WINDOW:]
    dv_ref[...] = dv[WINDOW:]


def window_fwd(factor, query, key, value, before):
    n, wide = query.shape
    here = pl.BlockSpec((n, DH), lambda h: (0, h))
    return call(
        functools.partial(window_fwd_kernel, factor),
        (wide // DH,),
        [here] * 5,
        here,
        jax.ShapeDtypeStruct((n, wide), BF16),
        4 * n * 2 * n * wide,
        12 * n * wide,
    )(query, before[0], key, before[1], value)


def window_bwd(factor, query, key, value, before, attn, grad):
    n, wide = query.shape
    here = pl.BlockSpec((n, DH), lambda h: (0, h))
    return call(
        functools.partial(window_bwd_kernel, factor),
        (wide // DH,),
        [here] * 7,
        [here] * 5,
        [
            jax.ShapeDtypeStruct((n, wide), BF16),
            jax.ShapeDtypeStruct((n, wide), F32),
            jax.ShapeDtypeStruct((n, wide), F32),
            jax.ShapeDtypeStruct((n, wide), BF16),
            jax.ShapeDtypeStruct((n, wide), BF16),
        ],
        10 * n * 2 * n * wide,
        28 * n * wide,
    )(query, before[0], key, before[1], value, attn, grad)


def body(
    win_query,
    win_key,
    win_value,
    clu_query,
    clu_key,
    clu_value,
    cluster_ids,
    win_gain,
    clu_gain,
    win_out_grad,
    clu_out_grad,
):
    n_rows = win_query.shape[0]
    factor = DH ** (-0.5)
    feat_width = (HW + HC) * DH
    sources = lax.axis_size("seq")
    n_cap = SLOTS // sources
    owned_count = 2 * n_rows // SLOTS
    pool_size = 2 * n_rows
    clu_heads = clu_query.shape[1] // DH
    rows = Rows(sources, owned_count, n_cap)

    def exchange(values):
        shaped = values.reshape(sources, pool_size // sources, values.shape[1])
        moved = lax.all_to_all(shaped, "seq", split_axis=0, concat_axis=0, tiled=True)
        return moved.reshape(values.shape)

    row_ids = lax.broadcasted_iota(jnp.int32, (n_rows, n_rows), 0)
    col_ids = lax.broadcasted_iota(jnp.int32, (n_rows, n_rows), 1)
    same_cluster = (cluster_ids[:, :, None] == cluster_ids[:, None, :]) & (col_ids < row_ids)
    rank_in = jnp.sum(same_cluster.astype(jnp.int32), axis=-1)
    slot_at = (cluster_ids * n_cap + rank_in)[:, None, :]

    chunks = CHUNKS if clu_heads % CHUNKS == 0 else 1
    per = clu_heads // chunks
    starts = [i * per for i in range(chunks)]

    sent_first = [
        dispatch(slot_at, [clu_query, clu_key, clu_value], first, per, pool_size, True)
        for first in starts
    ]
    before = (from_behind(win_key, "seq", 1), from_behind(win_value, "seq", 1))
    held = [exchange(part) for part in sent_first]
    attn_win = window_fwd(factor, win_query, win_key, win_value, before)
    held[0], attn_win = lax.optimization_barrier((held[0], attn_win))

    attn_held = [owner_call(owner_fwd_kernel, rows, factor, [qkv], 1) for qkv in held]
    attn_back = [exchange(part) for part in attn_held]
    attn_clu = ()
    for first, part in zip(starts, attn_back):
        attn_clu = collect(slot_at, part, first, per, 1, attn_clu)
    attn_clu = attn_clu[0]

    flat_win = attn_win.astype(F32)
    flat_clu = attn_clu.astype(F32)
    grad_win = win_out_grad.astype(F32) * win_gain
    grad_clu = clu_out_grad.astype(F32) * clu_gain
    totals = jnp.stack(
        [
            jnp.sum(flat_win * flat_win, axis=1) + jnp.sum(flat_clu * flat_clu, axis=1),
            jnp.sum(grad_win * flat_win, axis=1) + jnp.sum(grad_clu * flat_clu, axis=1),
        ]
    )
    totals = lax.psum(totals, "head")
    sq_total, dot_total = totals[0], totals[1]
    inv_rms = 1.0 / jnp.sqrt(sq_total / feat_width + EPSILON)
    coef_rows = inv_rms**3 * dot_total / feat_width
    dout_clu = (inv_rms[:, None] * grad_clu - coef_rows[:, None] * flat_clu).astype(BF16)
    dout_win = (inv_rms[:, None] * grad_win - coef_rows[:, None] * flat_win).astype(BF16)
    win_normed = (flat_win * inv_rms[:, None] * win_gain).astype(BF16)
    clu_normed = (flat_clu * inv_rms[:, None] * clu_gain).astype(BF16)

    grad_held = [
        exchange(dispatch(slot_at, [dout_clu], first, per, pool_size, False)) for first in starts
    ]
    win_dq, key_own, val_own, rim_key, rim_val = window_bwd(
        factor, win_query, win_key, win_value, before, attn_win, dout_win
    )
    grad_held[0], rim_key, rim_val = lax.optimization_barrier((grad_held[0], rim_key, rim_val))
    after_key = from_behind(rim_key, "seq", -1)
    after_val = from_behind(rim_val, "seq", -1)
    grad_held[-1], after_key, after_val = lax.optimization_barrier(
        (grad_held[-1], after_key, after_val)
    )

    clu_grads = ()
    sent = [
        owner_call(owner_bwd_kernel, rows, factor, [qkv, part, grad], 3)
        for qkv, part, grad in zip(held, attn_held, grad_held)
    ]
    home = [exchange(part) for part in sent]
    win_dk = ((key_own + after_key) * factor).astype(BF16)
    win_dv = (val_own + after_val).astype(BF16)
    for first, part in zip(starts, home):
        clu_grads = collect(slot_at, part, first, per, 3, clu_grads)
    return (win_normed, clu_normed, win_dq, win_dk, win_dv, *clu_grads)


def solution(mesh):
    return jax.shard_map(
        body,
        mesh=mesh,
        in_specs=(P("seq", "head"),) * 6
        + (P("head", "seq"), P("head"), P("head"))
        + (P("seq", "head"),) * 2,
        out_specs=(P("seq", "head"),) * 8,
        check_vma=False,
    )
```

```python
import functools

import jax
import jax.numpy as jnp
from jax import lax
from jax.experimental import pallas as pl
from jax.experimental.pallas import tpu as pltpu
from jax.sharding import PartitionSpec as P

HW = 32
HC = 32
DH = 128
WINDOW = 256
SLOTS = 128
CHUNKS = 2
GROUP = 4
EMPTY = 1000.0

EPSILON = 1e-06
F32 = jnp.float32
BF16 = jnp.bfloat16


def permuted(block, routes):
    size = lax.axis_size("seq")
    return lax.ppermute(block, "seq", [(a, b) for a, b in routes if 0 <= min(a, b) and max(a, b) < size])


def next_door(pair, step):
    size = lax.axis_size("seq")
    if size % GROUP or size == GROUP:
        return tuple(permuted(x, [(i, i + step) for i in range(size)]) for x in pair)
    bases = range(0, size, GROUP)
    leave, enter = (GROUP - 1, 0) if step > 0 else (0, GROUP - 1)
    place = lax.rem(lax.axis_index("seq"), GROUP)
    straight = [(i, i + step) for i in range(size) if i // GROUP == (i + step) // GROUP]
    near = [permuted(x, straight) for x in pair]
    parts = GROUP // 2
    rows = pair[0].shape[0] // parts
    pieces = [x[i * rows : (i + 1) * rows] for x in pair for i in range(parts)]
    spread = jnp.where(place == leave, pieces[leave], jnp.zeros_like(pieces[leave]))
    for p in range(GROUP):
        if p != leave:
            spread = spread + permuted(pieces[p], [(b + leave, b + p) for b in bases])
    crossed = permuted(spread, [(i, i + step * GROUP) for i in range(size)])
    landed = [
        crossed if p == enter else permuted(crossed, [(b + p, b + enter) for b in bases])
        for p in range(GROUP)
    ]
    far = [jnp.concatenate(landed[i * parts : (i + 1) * parts], axis=0) for i in range(2)]
    return tuple(jnp.where(place == enter, f, x) for f, x in zip(far, near))


def nt(a, b):
    return lax.dot_general(a, b, (((1,), (1,)), ((), ())), preferred_element_type=F32)


def tn(a, b):
    return lax.dot_general(a, b, (((0,), (0,)), ((), ())), preferred_element_type=F32)


def nn(a, b):
    return jnp.dot(a, b, preferred_element_type=F32)


def one_hot(slot_ref, pool):
    n = slot_ref.shape[-1]
    hit = lax.broadcasted_iota(jnp.int32, (pool, n), 0) == slot_ref[0]
    return jnp.where(hit, 1.0, 0.0).astype(BF16)


def normalized(scores, allowed):
    masked = jnp.where(allowed, scores, -jnp.inf)
    grown = jnp.exp(masked - jnp.max(masked, axis=-1, keepdims=True))
    return grown * (1.0 / jnp.sum(grown, axis=-1, keepdims=True))


def call(kernel, grid, in_specs, out_specs, out_shape, flops, size, **more):
    return pl.pallas_call(
        kernel,
        grid=grid,
        in_specs=in_specs,
        out_specs=out_specs,
        out_shape=out_shape,
        cost_estimate=pl.CostEstimate(flops=flops, bytes_accessed=size, transcendentals=0),
        compiler_params=pltpu.CompilerParams(vmem_limit_bytes=60 << 20),
        **more,
    )


def dispatch_kernel(mark, *refs):
    slot_ref, value_refs, out_ref = refs[0], refs[1:-1], refs[-1]
    picked = one_hot(slot_ref, out_ref.shape[0])
    for i, ref in enumerate(value_refs):
        moved = nn(picked, ref[...])
        if mark and i == len(value_refs) - 1:
            filled = nn(picked, jnp.ones(ref.shape, BF16))
            moved = jnp.where(filled > 0.5, moved, EMPTY)
        out_ref[:, i * DH : (i + 1) * DH] = moved.astype(BF16)


def dispatch(slot_at, values, first, count, pool, mark):
    n = slot_at.shape[-1]
    wide = len(values) * DH
    return call(
        functools.partial(dispatch_kernel, mark),
        (count,),
        [pl.BlockSpec((1, 1, n), lambda h: (h + first, 0, 0))]
        + [pl.BlockSpec((n, DH), lambda h: (0, h + first)) for _ in values],
        pl.BlockSpec((pool, wide), lambda h: (0, h)),
        jax.ShapeDtypeStruct((pool, count * wide), BF16),
        2 * count * pool * n * wide,
        2 * count * (pool + n) * wide,
    )(slot_at, *values)


def collect_kernel(n_out, *refs):
    slot_ref, rows_ref, out_refs = refs[0], refs[1], refs[-n_out:]
    picked = one_hot(slot_ref, rows_ref.shape[0])
    merged = tn(picked, rows_ref[...]).astype(BF16)
    for i, ref in enumerate(out_refs):
        ref[...] = merged[:, i * DH : (i + 1) * DH]


def collect(slot_at, rows, first, count, n_out, earlier):
    n = slot_at.shape[-1]
    pool = rows.shape[0]
    heads = slot_at.shape[0]
    wide = n_out * DH
    return call(
        functools.partial(collect_kernel, n_out),
        (count,),
        [
            pl.BlockSpec((1, 1, n), lambda h: (h + first, 0, 0)),
            pl.BlockSpec((pool, wide), lambda h: (0, h)),
        ]
        + [pl.BlockSpec(memory_space=pl.ANY) for _ in earlier],
        [pl.BlockSpec((n, DH), lambda h: (0, h + first))] * n_out,
        [jax.ShapeDtypeStruct((n, heads * DH), BF16)] * n_out,
        2 * count * pool * n * wide,
        2 * count * (pool + n) * wide,
        input_output_aliases={2 + i: i for i in range(len(earlier))},
    )(slot_at, rows, *earlier)


class Rows:
    def __init__(self, sources, owned, cap):
        self.sources, self.owned, self.cap = sources, owned, cap
        self.aligned = cap % 8 == 0

    def selector(self, c):
        members = self.sources * self.cap
        layout = (members, members * self.owned)
        member = lax.broadcasted_iota(jnp.int32, layout, 0)
        row = lax.broadcasted_iota(jnp.int32, layout, 1)
        want = member // self.cap * (self.cap * self.owned) + c * self.cap + member % self.cap
        return jnp.where(row == want, 1.0, 0.0).astype(BF16)

    def split(self, rows):
        members = self.sources * self.cap
        if not self.aligned:
            return [nn(self.selector(c), rows).astype(BF16) for c in range(self.owned)]
        wide = rows.shape[1]
        four = rows.astype(F32).reshape(self.sources, self.owned, self.cap, wide)
        return [four[:, c].reshape(members, wide).astype(BF16) for c in range(self.owned)]

    def join(self, parts):
        wide = parts[0].shape[1]
        pool = self.sources * self.cap * self.owned
        if not self.aligned:
            total = jnp.zeros((pool, wide), F32)
            for c, part in enumerate(parts):
                total = total + tn(self.selector(c), part.astype(BF16))
            return total.astype(BF16)
        shaped = [p.reshape(self.sources, 1, self.cap, wide) for p in parts]
        return jnp.concatenate(shaped, axis=1).reshape(pool, wide).astype(BF16)


def cluster_allowed(v):
    members = v.shape[0]
    lane = lax.broadcasted_iota(jnp.int32, (8, DH), 1)
    first = nt(jnp.where(lane == 0, 1.0, 0.0).astype(BF16), v)[:1]
    row = lax.broadcasted_iota(jnp.int32, (members, members), 0)
    col = lax.broadcasted_iota(jnp.int32, (members, members), 1)
    live = jnp.broadcast_to(first, (members, members)) < EMPTY / 2
    return (live & (col <= row)) | (col == row)


def owner_fwd_kernel(rows, factor, qkv_ref, out_ref):
    parts = []
    for qkv in rows.split(qkv_ref[...]):
        q, k, v = qkv[:, :DH], qkv[:, DH : 2 * DH], qkv[:, 2 * DH :]
        prob = normalized(nt(q, k) * factor, cluster_allowed(v))
        parts.append(nn(prob.astype(BF16), v))
    out_ref[...] = rows.join(parts)


def owner_bwd_kernel(rows, factor, qkv_ref, attn_ref, grad_ref, out_ref):
    attn_parts = rows.split(attn_ref[...])
    grad_parts = rows.split(grad_ref[...])
    parts = []
    for c, qkv in enumerate(rows.split(qkv_ref[...])):
        q, k, v = qkv[:, :DH], qkv[:, DH : 2 * DH], qkv[:, 2 * DH :]
        grad = grad_parts[c]
        row_dot = jnp.sum(grad.astype(F32) * attn_parts[c].astype(F32), axis=-1, keepdims=True)
        prob = normalized(nt(q, k) * factor, cluster_allowed(v))
        change = (prob * (nt(grad, v) - row_dot)).astype(BF16)
        dq = nn(change, k) * factor
        dk = tn(change, q) * factor
        dv = tn(prob.astype(BF16), grad)
        parts.append(jnp.concatenate([dq, dk, dv], axis=1))
    out_ref[...] = rows.join(parts)


def owner_call(kernel, rows, factor, arrays, n_out):
    pool = arrays[0].shape[0]
    count = arrays[0].shape[1] // (3 * DH)
    members = rows.sources * rows.cap
    wides = [a.shape[1] // count for a in arrays]
    return call(
        functools.partial(kernel, rows, factor),
        (count,),
        [pl.BlockSpec((pool, w), lambda h: (0, h)) for w in wides],
        pl.BlockSpec((pool, n_out * DH), lambda h: (0, h)),
        jax.ShapeDtypeStruct((pool, count * n_out * DH), BF16),
        12 * count * pool * members * DH,
        2 * count * pool * (sum(wides) + n_out * DH),
    )(*arrays)


def window_prob(factor, q, keys):
    n = q.shape[0]
    row = lax.broadcasted_iota(jnp.int32, (n, n + WINDOW), 0)
    col = lax.broadcasted_iota(jnp.int32, (n, n + WINDOW), 1)
    gap = row + WINDOW - col
    lowest = jnp.where(lax.axis_index("seq") > 0, 0, WINDOW)
    allowed = (gap >= 0) & (gap < WINDOW) & (col >= lowest)
    return normalized(nt(q, keys) * factor, allowed)


def window_fwd_kernel(factor, q_ref, kp_ref, k_ref, vp_ref, v_ref, out_ref):
    keys = jnp.concatenate([kp_ref[...], k_ref[...]], axis=0)
    vals = jnp.concatenate([vp_ref[...], v_ref[...]], axis=0)
    prob = window_prob(factor, q_ref[...], keys)
    out_ref[...] = nn(prob.astype(BF16), vals).astype(BF16)


def window_bwd_kernel(
    factor, q_ref, kp_ref, k_ref, vp_ref, v_ref, attn_ref, grad_ref, dq_ref, dk_ref, dv_ref, rim_key_ref, rim_val_ref
):
    q, grad = q_ref[...], grad_ref[...]
    keys = jnp.concatenate([kp_ref[...], k_ref[...]], axis=0)
    vals = jnp.concatenate([vp_ref[...], v_ref[...]], axis=0)
    prob = window_prob(factor, q, keys)
    row_dot = jnp.sum(grad.astype(F32) * attn_ref[...].astype(F32), axis=-1, keepdims=True)
    change = (prob * (nt(grad, vals) - row_dot)).astype(BF16)
    dq_ref[...] = (nn(change, keys) * factor).astype(BF16)
    dk = tn(change, q)
    dv = tn(prob.astype(BF16), grad)
    rim_key_ref[...] = dk[:WINDOW].astype(BF16)
    rim_val_ref[...] = dv[:WINDOW].astype(BF16)
    dk_ref[...] = dk[WINDOW:]
    dv_ref[...] = dv[WINDOW:]


def window_fwd(factor, query, key, value, before):
    n, wide = query.shape
    here = pl.BlockSpec((n, DH), lambda h: (0, h))
    return call(
        functools.partial(window_fwd_kernel, factor),
        (wide // DH,),
        [here] * 5,
        here,
        jax.ShapeDtypeStruct((n, wide), BF16),
        4 * n * 2 * n * wide,
        12 * n * wide,
    )(query, before[0], key, before[1], value)


def window_bwd(factor, query, key, value, before, attn, grad):
    n, wide = query.shape
    here = pl.BlockSpec((n, DH), lambda h: (0, h))
    return call(
        functools.partial(window_bwd_kernel, factor),
        (wide // DH,),
        [here] * 7,
        [here] * 5,
        [
            jax.ShapeDtypeStruct((n, wide), BF16),
            jax.ShapeDtypeStruct((n, wide), F32),
            jax.ShapeDtypeStruct((n, wide), F32),
            jax.ShapeDtypeStruct((n, wide), BF16),
            jax.ShapeDtypeStruct((n, wide), BF16),
        ],
        10 * n * 2 * n * wide,
        28 * n * wide,
    )(query, before[0], key, before[1], value, attn, grad)


def body(
    win_query,
    win_key,
    win_value,
    clu_query,
    clu_key,
    clu_value,
    cluster_ids,
    win_gain,
    clu_gain,
    win_out_grad,
    clu_out_grad,
):
    n_rows = win_query.shape[0]
    factor = DH ** (-0.5)
    feat_width = (HW + HC) * DH
    sources = lax.axis_size("seq")
    n_cap = SLOTS // sources
    owned_count = 2 * n_rows // SLOTS
    pool_size = 2 * n_rows
    clu_heads = clu_query.shape[1] // DH
    rows = Rows(sources, owned_count, n_cap)

    def exchange(values):
        shaped = values.reshape(sources, pool_size // sources, values.shape[1])
        moved = lax.all_to_all(shaped, "seq", split_axis=0, concat_axis=0, tiled=True)
        return moved.reshape(values.shape)

    row_ids = lax.broadcasted_iota(jnp.int32, (n_rows, n_rows), 0)
    col_ids = lax.broadcasted_iota(jnp.int32, (n_rows, n_rows), 1)
    same_cluster = (cluster_ids[:, :, None] == cluster_ids[:, None, :]) & (col_ids < row_ids)
    rank_in = jnp.sum(same_cluster.astype(jnp.int32), axis=-1)
    slot_at = (cluster_ids * n_cap + rank_in)[:, None, :]

    chunks = CHUNKS if clu_heads % CHUNKS == 0 else 1
    per = clu_heads // chunks
    starts = [i * per for i in range(chunks)]

    sent_first = [
        dispatch(slot_at, [clu_query, clu_key, clu_value], first, per, pool_size, True)
        for first in starts
    ]
    before = next_door((win_key, win_value), 1)
    sent_first[-1], before = lax.optimization_barrier((sent_first[-1], before))
    held = [exchange(part) for part in sent_first]
    attn_win = window_fwd(factor, win_query, win_key, win_value, before)
    held[0], attn_win = lax.optimization_barrier((held[0], attn_win))

    attn_held = [owner_call(owner_fwd_kernel, rows, factor, [qkv], 1) for qkv in held]
    attn_back = [exchange(part) for part in attn_held]
    attn_clu = ()
    for first, part in zip(starts, attn_back):
        attn_clu = collect(slot_at, part, first, per, 1, attn_clu)
    attn_clu = attn_clu[0]

    flat_win = attn_win.astype(F32)
    flat_clu = attn_clu.astype(F32)
    grad_win = win_out_grad.astype(F32) * win_gain
    grad_clu = clu_out_grad.astype(F32) * clu_gain
    totals = jnp.stack(
        [
            jnp.sum(flat_win * flat_win, axis=1) + jnp.sum(flat_clu * flat_clu, axis=1),
            jnp.sum(grad_win * flat_win, axis=1) + jnp.sum(grad_clu * flat_clu, axis=1),
        ]
    )
    totals = lax.psum(totals, "head")
    sq_total, dot_total = totals[0], totals[1]
    inv_rms = 1.0 / jnp.sqrt(sq_total / feat_width + EPSILON)
    coef_rows = inv_rms**3 * dot_total / feat_width
    dout_clu = (inv_rms[:, None] * grad_clu - coef_rows[:, None] * flat_clu).astype(BF16)
    dout_win = (inv_rms[:, None] * grad_win - coef_rows[:, None] * flat_win).astype(BF16)
    win_normed = (flat_win * inv_rms[:, None] * win_gain).astype(BF16)
    clu_normed = (flat_clu * inv_rms[:, None] * clu_gain).astype(BF16)

    grad_held = [
        exchange(dispatch(slot_at, [dout_clu], first, per, pool_size, False)) for first in starts
    ]
    win_dq, key_own, val_own, rim_key, rim_val = window_bwd(
        factor, win_query, win_key, win_value, before, attn_win, dout_win
    )
    grad_held[0], rim_key, rim_val = lax.optimization_barrier((grad_held[0], rim_key, rim_val))
    after_key, after_val = next_door((rim_key, rim_val), -1)
    clu_grads = ()
    sent = [
        owner_call(owner_bwd_kernel, rows, factor, [qkv, part, grad], 3)
        for qkv, part, grad in zip(held, attn_held, grad_held)
    ]
    sent[-1], after_key, after_val = lax.optimization_barrier((sent[-1], after_key, after_val))
    home = [exchange(part) for part in sent]
    win_dk = ((key_own + after_key) * factor).astype(BF16)
    win_dv = (val_own + after_val).astype(BF16)
    for first, part in zip(starts, home):
        clu_grads = collect(slot_at, part, first, per, 3, clu_grads)
    return (win_normed, clu_normed, win_dq, win_dk, win_dv, *clu_grads)


def solution(mesh):
    return jax.shard_map(
        body,
        mesh=mesh,
        in_specs=(P("seq", "head"),) * 6
        + (P("head", "seq"), P("head"), P("head"))
        + (P("seq", "head"),) * 2,
        out_specs=(P("seq", "head"),) * 8,
        check_vma=False,
    )
```

```python
import functools

import jax
import jax.numpy as jnp
from jax import lax
from jax.experimental import pallas as pl
from jax.experimental.pallas import tpu as pltpu
from jax.sharding import PartitionSpec as P

HW = 32
HC = 32
DH = 128
WINDOW = 256
SLOTS = 128
CHUNKS = 2
GROUP = 4
EMPTY = 1000.0

EPSILON = 1e-06
F32 = jnp.float32
BF16 = jnp.bfloat16


def permuted(block, routes):
    size = lax.axis_size("seq")
    return lax.ppermute(block, "seq", [(a, b) for a, b in routes if 0 <= min(a, b) and max(a, b) < size])


def next_door(pair, step, meet):
    size = lax.axis_size("seq")
    if size % GROUP or size == GROUP:
        return tuple(permuted(x, [(i, i + step) for i in range(size)]) for x in pair)
    bases = range(0, size, GROUP)
    leave, enter = (GROUP - 1, 0) if step > 0 else (0, GROUP - 1)
    place = lax.rem(lax.axis_index("seq"), GROUP)
    straight = [(i, i + step) for i in range(size) if i // GROUP == (i + step) // GROUP]
    near = [permuted(x, straight) for x in pair]
    parts = GROUP // 2
    rows = pair[0].shape[0] // parts
    pieces = [x[i * rows : (i + 1) * rows] for x in pair for i in range(parts)]
    spread = jnp.where(place == leave, pieces[leave], jnp.zeros_like(pieces[leave]))
    for p in range(GROUP):
        if p != leave:
            spread = spread + permuted(pieces[p], [(b + leave, b + p) for b in bases])
    near, spread = meet(near, spread)
    crossed = permuted(spread, [(i, i + step * GROUP) for i in range(size)])
    landed = [
        crossed if p == enter else permuted(crossed, [(b + p, b + enter) for b in bases])
        for p in range(GROUP)
    ]
    far = [jnp.concatenate(landed[i * parts : (i + 1) * parts], axis=0) for i in range(2)]
    return tuple(jnp.where(place == enter, f, x) for f, x in zip(far, near))


def nt(a, b):
    return lax.dot_general(a, b, (((1,), (1,)), ((), ())), preferred_element_type=F32)


def tn(a, b):
    return lax.dot_general(a, b, (((0,), (0,)), ((), ())), preferred_element_type=F32)


def nn(a, b):
    return jnp.dot(a, b, preferred_element_type=F32)


def one_hot(slot_ref, pool):
    n = slot_ref.shape[-1]
    hit = lax.broadcasted_iota(jnp.int32, (pool, n), 0) == slot_ref[0]
    return jnp.where(hit, 1.0, 0.0).astype(BF16)


def normalized(scores, allowed):
    masked = jnp.where(allowed, scores, -jnp.inf)
    grown = jnp.exp(masked - jnp.max(masked, axis=-1, keepdims=True))
    return grown * (1.0 / jnp.sum(grown, axis=-1, keepdims=True))


def call(kernel, grid, in_specs, out_specs, out_shape, flops, size, **more):
    return pl.pallas_call(
        kernel,
        grid=grid,
        in_specs=in_specs,
        out_specs=out_specs,
        out_shape=out_shape,
        cost_estimate=pl.CostEstimate(flops=flops, bytes_accessed=size, transcendentals=0),
        compiler_params=pltpu.CompilerParams(vmem_limit_bytes=60 << 20),
        **more,
    )


def dispatch_kernel(mark, *refs):
    slot_ref, value_refs, out_ref = refs[0], refs[1:-1], refs[-1]
    picked = one_hot(slot_ref, out_ref.shape[0])
    for i, ref in enumerate(value_refs):
        moved = nn(picked, ref[...])
        if mark and i == len(value_refs) - 1:
            filled = nn(picked, jnp.ones(ref.shape, BF16))
            moved = jnp.where(filled > 0.5, moved, EMPTY)
        out_ref[:, i * DH : (i + 1) * DH] = moved.astype(BF16)


def dispatch(slot_at, values, first, count, pool, mark):
    n = slot_at.shape[-1]
    wide = len(values) * DH
    return call(
        functools.partial(dispatch_kernel, mark),
        (count,),
        [pl.BlockSpec((1, 1, n), lambda h: (h + first, 0, 0))]
        + [pl.BlockSpec((n, DH), lambda h: (0, h + first)) for _ in values],
        pl.BlockSpec((pool, wide), lambda h: (0, h)),
        jax.ShapeDtypeStruct((pool, count * wide), BF16),
        2 * count * pool * n * wide,
        2 * count * (pool + n) * wide,
    )(slot_at, *values)


def collect_kernel(n_out, *refs):
    slot_ref, rows_ref, out_refs = refs[0], refs[1], refs[-n_out:]
    picked = one_hot(slot_ref, rows_ref.shape[0])
    merged = tn(picked, rows_ref[...]).astype(BF16)
    for i, ref in enumerate(out_refs):
        ref[...] = merged[:, i * DH : (i + 1) * DH]


def collect(slot_at, rows, first, count, n_out, earlier):
    n = slot_at.shape[-1]
    pool = rows.shape[0]
    heads = slot_at.shape[0]
    wide = n_out * DH
    return call(
        functools.partial(collect_kernel, n_out),
        (count,),
        [
            pl.BlockSpec((1, 1, n), lambda h: (h + first, 0, 0)),
            pl.BlockSpec((pool, wide), lambda h: (0, h)),
        ]
        + [pl.BlockSpec(memory_space=pl.ANY) for _ in earlier],
        [pl.BlockSpec((n, DH), lambda h: (0, h + first))] * n_out,
        [jax.ShapeDtypeStruct((n, heads * DH), BF16)] * n_out,
        2 * count * pool * n * wide,
        2 * count * (pool + n) * wide,
        input_output_aliases={2 + i: i for i in range(len(earlier))},
    )(slot_at, rows, *earlier)


class Rows:
    def __init__(self, sources, owned, cap):
        self.sources, self.owned, self.cap = sources, owned, cap
        self.aligned = cap % 8 == 0

    def selector(self, c):
        members = self.sources * self.cap
        layout = (members, members * self.owned)
        member = lax.broadcasted_iota(jnp.int32, layout, 0)
        row = lax.broadcasted_iota(jnp.int32, layout, 1)
        want = member // self.cap * (self.cap * self.owned) + c * self.cap + member % self.cap
        return jnp.where(row == want, 1.0, 0.0).astype(BF16)

    def split(self, rows):
        members = self.sources * self.cap
        if not self.aligned:
            return [nn(self.selector(c), rows).astype(BF16) for c in range(self.owned)]
        wide = rows.shape[1]
        four = rows.astype(F32).reshape(self.sources, self.owned, self.cap, wide)
        return [four[:, c].reshape(members, wide).astype(BF16) for c in range(self.owned)]

    def join(self, parts):
        wide = parts[0].shape[1]
        pool = self.sources * self.cap * self.owned
        if not self.aligned:
            total = jnp.zeros((pool, wide), F32)
            for c, part in enumerate(parts):
                total = total + tn(self.selector(c), part.astype(BF16))
            return total.astype(BF16)
        shaped = [p.reshape(self.sources, 1, self.cap, wide) for p in parts]
        return jnp.concatenate(shaped, axis=1).reshape(pool, wide).astype(BF16)


def cluster_allowed(v):
    members = v.shape[0]
    lane = lax.broadcasted_iota(jnp.int32, (8, DH), 1)
    first = nt(jnp.where(lane == 0, 1.0, 0.0).astype(BF16), v)[:1]
    row = lax.broadcasted_iota(jnp.int32, (members, members), 0)
    col = lax.broadcasted_iota(jnp.int32, (members, members), 1)
    live = jnp.broadcast_to(first, (members, members)) < EMPTY / 2
    return (live & (col <= row)) | (col == row)


def owner_fwd_kernel(rows, factor, qkv_ref, out_ref):
    parts = []
    for qkv in rows.split(qkv_ref[...]):
        q, k, v = qkv[:, :DH], qkv[:, DH : 2 * DH], qkv[:, 2 * DH :]
        prob = normalized(nt(q, k) * factor, cluster_allowed(v))
        parts.append(nn(prob.astype(BF16), v))
    out_ref[...] = rows.join(parts)


def owner_bwd_kernel(rows, factor, qkv_ref, attn_ref, grad_ref, out_ref):
    attn_parts = rows.split(attn_ref[...])
    grad_parts = rows.split(grad_ref[...])
    parts = []
    for c, qkv in enumerate(rows.split(qkv_ref[...])):
        q, k, v = qkv[:, :DH], qkv[:, DH : 2 * DH], qkv[:, 2 * DH :]
        grad = grad_parts[c]
        row_dot = jnp.sum(grad.astype(F32) * attn_parts[c].astype(F32), axis=-1, keepdims=True)
        prob = normalized(nt(q, k) * factor, cluster_allowed(v))
        change = (prob * (nt(grad, v) - row_dot)).astype(BF16)
        dq = nn(change, k) * factor
        dk = tn(change, q) * factor
        dv = tn(prob.astype(BF16), grad)
        parts.append(jnp.concatenate([dq, dk, dv], axis=1))
    out_ref[...] = rows.join(parts)


def owner_call(kernel, rows, factor, arrays, n_out):
    pool = arrays[0].shape[0]
    count = arrays[0].shape[1] // (3 * DH)
    members = rows.sources * rows.cap
    wides = [a.shape[1] // count for a in arrays]
    return call(
        functools.partial(kernel, rows, factor),
        (count,),
        [pl.BlockSpec((pool, w), lambda h: (0, h)) for w in wides],
        pl.BlockSpec((pool, n_out * DH), lambda h: (0, h)),
        jax.ShapeDtypeStruct((pool, count * n_out * DH), BF16),
        12 * count * pool * members * DH,
        2 * count * pool * (sum(wides) + n_out * DH),
    )(*arrays)


def window_prob(factor, q, keys):
    n = q.shape[0]
    row = lax.broadcasted_iota(jnp.int32, (n, n + WINDOW), 0)
    col = lax.broadcasted_iota(jnp.int32, (n, n + WINDOW), 1)
    gap = row + WINDOW - col
    lowest = jnp.where(lax.axis_index("seq") > 0, 0, WINDOW)
    allowed = (gap >= 0) & (gap < WINDOW) & (col >= lowest)
    return normalized(nt(q, keys) * factor, allowed)


def window_fwd_kernel(factor, q_ref, kp_ref, k_ref, vp_ref, v_ref, out_ref):
    keys = jnp.concatenate([kp_ref[...], k_ref[...]], axis=0)
    vals = jnp.concatenate([vp_ref[...], v_ref[...]], axis=0)
    prob = window_prob(factor, q_ref[...], keys)
    out_ref[...] = nn(prob.astype(BF16), vals).astype(BF16)


def window_bwd_kernel(
    factor, q_ref, kp_ref, k_ref, vp_ref, v_ref, attn_ref, grad_ref, dq_ref, dk_ref, dv_ref, rim_key_ref, rim_val_ref
):
    q, grad = q_ref[...], grad_ref[...]
    keys = jnp.concatenate([kp_ref[...], k_ref[...]], axis=0)
    vals = jnp.concatenate([vp_ref[...], v_ref[...]], axis=0)
    prob = window_prob(factor, q, keys)
    row_dot = jnp.sum(grad.astype(F32) * attn_ref[...].astype(F32), axis=-1, keepdims=True)
    change = (prob * (nt(grad, vals) - row_dot)).astype(BF16)
    dq_ref[...] = (nn(change, keys) * factor).astype(BF16)
    dk = tn(change, q)
    dv = tn(prob.astype(BF16), grad)
    rim_key_ref[...] = dk[:WINDOW].astype(BF16)
    rim_val_ref[...] = dv[:WINDOW].astype(BF16)
    dk_ref[...] = dk[WINDOW:]
    dv_ref[...] = dv[WINDOW:]


def window_fwd(factor, query, key, value, before):
    n, wide = query.shape
    here = pl.BlockSpec((n, DH), lambda h: (0, h))
    return call(
        functools.partial(window_fwd_kernel, factor),
        (wide // DH,),
        [here] * 5,
        here,
        jax.ShapeDtypeStruct((n, wide), BF16),
        4 * n * 2 * n * wide,
        12 * n * wide,
    )(query, before[0], key, before[1], value)


def window_bwd(factor, query, key, value, before, attn, grad):
    n, wide = query.shape
    here = pl.BlockSpec((n, DH), lambda h: (0, h))
    return call(
        functools.partial(window_bwd_kernel, factor),
        (wide // DH,),
        [here] * 7,
        [here] * 5,
        [
            jax.ShapeDtypeStruct((n, wide), BF16),
            jax.ShapeDtypeStruct((n, wide), F32),
            jax.ShapeDtypeStruct((n, wide), F32),
            jax.ShapeDtypeStruct((n, wide), BF16),
            jax.ShapeDtypeStruct((n, wide), BF16),
        ],
        10 * n * 2 * n * wide,
        28 * n * wide,
    )(query, before[0], key, before[1], value, attn, grad)


def body(
    win_query,
    win_key,
    win_value,
    clu_query,
    clu_key,
    clu_value,
    cluster_ids,
    win_gain,
    clu_gain,
    win_out_grad,
    clu_out_grad,
):
    n_rows = win_query.shape[0]
    factor = DH ** (-0.5)
    feat_width = (HW + HC) * DH
    sources = lax.axis_size("seq")
    n_cap = SLOTS // sources
    owned_count = 2 * n_rows // SLOTS
    pool_size = 2 * n_rows
    clu_heads = clu_query.shape[1] // DH
    rows = Rows(sources, owned_count, n_cap)

    def exchange(values):
        shaped = values.reshape(sources, pool_size // sources, values.shape[1])
        moved = lax.all_to_all(shaped, "seq", split_axis=0, concat_axis=0, tiled=True)
        return moved.reshape(values.shape)

    row_ids = lax.broadcasted_iota(jnp.int32, (n_rows, n_rows), 0)
    col_ids = lax.broadcasted_iota(jnp.int32, (n_rows, n_rows), 1)
    same_cluster = (cluster_ids[:, :, None] == cluster_ids[:, None, :]) & (col_ids < row_ids)
    rank_in = jnp.sum(same_cluster.astype(jnp.int32), axis=-1)
    slot_at = (cluster_ids * n_cap + rank_in)[:, None, :]

    chunks = CHUNKS if clu_heads % CHUNKS == 0 else 1
    per = clu_heads // chunks
    starts = [i * per for i in range(chunks)]

    sent_first = [
        dispatch(slot_at, [clu_query, clu_key, clu_value], first, per, pool_size, True)
        for first in starts
    ]

    def meet_second_exchange(near, spread):
        sent_first[-1], near, spread = lax.optimization_barrier((sent_first[-1], near, spread))
        return near, spread

    before = next_door((win_key, win_value), 1, meet_second_exchange)
    held = [exchange(part) for part in sent_first]

    attn_held = [owner_call(owner_fwd_kernel, rows, factor, [qkv], 1) for qkv in held]
    attn_held[0], before = lax.optimization_barrier((attn_held[0], before))
    attn_back = [exchange(part) for part in attn_held]
    attn_win = window_fwd(factor, win_query, win_key, win_value, before)
    attn_back[0], attn_win = lax.optimization_barrier((attn_back[0], attn_win))
    attn_clu = ()
    for first, part in zip(starts, attn_back):
        attn_clu = collect(slot_at, part, first, per, 1, attn_clu)
    attn_clu = attn_clu[0]

    flat_win = attn_win.astype(F32)
    flat_clu = attn_clu.astype(F32)
    grad_win = win_out_grad.astype(F32) * win_gain
    grad_clu = clu_out_grad.astype(F32) * clu_gain
    totals = jnp.stack(
        [
            jnp.sum(flat_win * flat_win, axis=1) + jnp.sum(flat_clu * flat_clu, axis=1),
            jnp.sum(grad_win * flat_win, axis=1) + jnp.sum(grad_clu * flat_clu, axis=1),
        ]
    )
    totals = lax.psum(totals, "head")
    sq_total, dot_total = totals[0], totals[1]
    inv_rms = 1.0 / jnp.sqrt(sq_total / feat_width + EPSILON)
    coef_rows = inv_rms**3 * dot_total / feat_width
    dout_clu = (inv_rms[:, None] * grad_clu - coef_rows[:, None] * flat_clu).astype(BF16)
    dout_win = (inv_rms[:, None] * grad_win - coef_rows[:, None] * flat_win).astype(BF16)
    win_normed = (flat_win * inv_rms[:, None] * win_gain).astype(BF16)
    clu_normed = (flat_clu * inv_rms[:, None] * clu_gain).astype(BF16)

    grad_held = [
        exchange(dispatch(slot_at, [dout_clu], first, per, pool_size, False)) for first in starts
    ]
    win_dq, key_own, val_own, rim_key, rim_val = window_bwd(
        factor, win_query, win_key, win_value, before, attn_win, dout_win
    )
    grad_held[0], rim_key, rim_val = lax.optimization_barrier((grad_held[0], rim_key, rim_val))
    clu_grads = ()
    sent = [
        owner_call(owner_bwd_kernel, rows, factor, [qkv, part, grad], 3)
        for qkv, part, grad in zip(held, attn_held, grad_held)
    ]

    def meet_last_exchange(near, spread):
        sent[-1], near, spread = lax.optimization_barrier((sent[-1], near, spread))
        return near, spread

    after_key, after_val = next_door((rim_key, rim_val), -1, meet_last_exchange)
    home = [exchange(part) for part in sent]
    home[0], after_key, after_val = lax.optimization_barrier((home[0], after_key, after_val))
    win_dk = ((key_own + after_key) * factor).astype(BF16)
    win_dv = (val_own + after_val).astype(BF16)
    for first, part in zip(starts, home):
        clu_grads = collect(slot_at, part, first, per, 3, clu_grads)
    return (win_normed, clu_normed, win_dq, win_dk, win_dv, *clu_grads)


def solution(mesh):
    return jax.shard_map(
        body,
        mesh=mesh,
        in_specs=(P("seq", "head"),) * 6
        + (P("head", "seq"), P("head"), P("head"))
        + (P("seq", "head"),) * 2,
        out_specs=(P("seq", "head"),) * 8,
        check_vma=False,
    )
```
